32 devices in a mesh: dp: 4 (over z), expert: 8 (over y, x, core).
Axes of the slice: x: 2, y: 2, z: 4, core: 2. Of those that a mesh axis runs over, the one named last changes fastest.
Arguments:
- tokens: bfloat16 [4096, 2048], P(('dp', 'expert')), may hold values from -6 to 6
- routes: int32 [4096, 4], P(('dp', 'expert')), may hold values from 0 to 7, all different within a row; in each aligned block of 128 rows (0 to 127, 128 to 255, ...) at most 80 rows name the same one
- gates: float32 [4096, 4], P(('dp', 'expert')), may hold values from 0.05 to 0.5
- gate_up: bfloat16 [8, 2048, 2816], P('expert'), may hold values from -0.125 to 0.125
- down_proj: bfloat16 [8, 1408, 2048], P('expert'), may hold values from -0.15625 to 0.15625
- projection: bfloat16 [2048, 512], replicated, may hold values from -0.125 to 0.125
- matches: int32 [32, 128], P(('dp', 'expert')), may hold values from 0 to 127, each once within a row
Outputs:
- grad_tokens: bfloat16 [4096, 2048], P(('dp', 'expert'))
- grad_projection: float32 [2048, 512], P(('dp', 'expert'))
- row_loss: float32 [4096], P(('dp', 'expert'))
The draws below stay inside these ranges and needn't reach their ends.
Inputs may be any that keep to these rules, and one draw needn't show every extreme that they name: `routes`: each row names 4 different experts; within the rows of one device no expert is named more than 80 times, a bound that some block reaches. `matches`: within each patch the entries are a permutation of 0 to 127.
All inputs are finite; a program needn't handle non-finite values.
Results may differ from the reference program's by a relative error of at most 0.011.
Values may be sent and summed in bfloat16 or wider, within the bound.
A program may use at most 128 MiB of HBM per device.

```python
import math
import jax
import jax.numpy as jnp
import numpy as np
from jax import lax

D = 2048
FFH = 1408
EMB = 512
TOP = 4
PATCH = 128
TOK_DEV = 128
EXPERTS = 8
CAP = 80
TOKENS = 4096
PATCHES = 32
N_DP = 4
N_EXPERT = 8


def spiked(drawn, stream_key, source, target, blocks, factor):
    owner, partner = [(jnp.arange(drawn.shape[dim]) // (drawn.shape[dim] // blocks)).reshape([-1 if axis == dim else 1 for axis in range(drawn.ndim)]) for dim in (source, target)]
    chosen = jax.random.permutation(stream_key, blocks)[partner]
    strong = (owner == chosen) | (owner == (partner + blocks // 2) % blocks)
    return jnp.where(strong, factor * drawn, drawn)


def levels(own_key, shape, split, smallest, high):
    gain = 1.0
    for axis_at, blocks in split:
        draws = jax.random.uniform(jax.random.fold_in(jax.random.fold_in(own_key, 6), axis_at), (blocks,), jnp.float32, smallest / len(split), high / len(split))
        gain = gain * jnp.repeat(jnp.exp(draws), shape[axis_at] // blocks).reshape((-1,) + (1,) * (len(shape) - 1 - axis_at))
    return gain


def shared_out(rng, own, number, rows, count, top, limit, slope):
    order = jax.random.permutation(rng, count)
    packed, usual = load_shares(count, rows * top, limit, slope, True), load_shares(count, rows * top, limit, slope, False)
    places = jnp.arange(count)

    def named(lengths, rotation):
        used = int((lengths > 0).sum())
        fixed = max(1, used // 4)
        shifted = fixed + (places - fixed + rotation * (used - fixed)) % max(1, count - fixed)
        return jnp.zeros((count,), jnp.int32).at[order[jnp.where(places < fixed, places, shifted)]].set(jnp.asarray(lengths, jnp.int32))

    lengths = jnp.where(number % 4 == 0, named(packed, number // 4), named(usual, number - number // 4 - 1))
    mixed = jax.random.permutation(jax.random.fold_in(own, 3), count)
    source_of, receiver = mixed[0:count // 2 * 2:2], mixed[1:count // 2 * 2:2]
    margin = jnp.minimum(lengths[source_of] - 1, limit - lengths[receiver]) // 2
    margin = jnp.where((source_of == order[0]) | (receiver == order[0]) | (lengths[receiver] == 0), 0, jnp.maximum(margin, 0))
    shifted = jax.random.randint(jax.random.fold_in(own, 4), (count // 2,), 0, 1 << 20) % (margin + 1)
    lengths = lengths.at[source_of].add(-shifted).at[receiver].add(shifted)
    items = jnp.searchsorted(jnp.cumsum(lengths), jnp.arange(rows * top), side="right").astype(jnp.int32)
    listing = items.reshape(top, rows).T
    listing = listing[jax.random.permutation(jax.random.fold_in(own, 1), rows)]
    rotation = jax.random.randint(jax.random.fold_in(own, 2), (rows, 1), 0, top)
    return jnp.take_along_axis(listing, (jnp.arange(top)[None, :] + rotation) % top, axis=1)


def load_shares(count, total, limit, slope, full):
    loads = [(1 << 20) // math.isqrt(rank ** slope) + 1 for rank in range(1, count + 1)]
    largest = limit if full else min(limit, max(-(-total // count), total * loads[0] // sum(loads)))
    least = 1 if total - largest >= count - 1 else 0
    holding, rest = [largest] + [least] * (count - 1), total - largest - least * (count - 1)
    while rest > 0:
        free = [i for i in range(1, count) if holding[i] < largest] or [i for i in range(1, count) if holding[i] < limit]
        whole, left = sum([loads[i] for i in free]), rest
        for i in free:
            extra = min(limit - holding[i], max(1, left * loads[i] // whole), rest)
            holding[i] = holding[i] + extra
            rest = rest - extra
    return np.array(holding)


def noise(own_key, extent, scale, limit, split=(), kind=jnp.bfloat16):
    factor_of = levels(own_key, extent, split, -0.22, 0.18) if split else 1.0
    drawn = jax.random.normal(own_key, extent, jnp.float32) * scale * factor_of
    return jnp.minimum(jnp.maximum(drawn, -limit), limit).astype(kind)


def heavy_noise(key, shape, width, bound, pieces, heavy, kind=jnp.bfloat16):
    values = width * jax.random.normal(key, shape, jnp.float32)
    if pieces:
        values = values * levels(key, shape, pieces, -0.22, 0.18)
    return jnp.clip(spiked(values, jax.random.fold_in(key, 3), *heavy), -bound, bound).astype(kind)


def setup_inputs(seed: int = 0) -> dict:
    key_list = jax.random.split(jax.random.key(seed), 8)
    tokens = heavy_noise(key_list[0], (TOKENS, D), 1.0, 6.0, ((0, 32),), (0, 1, 32, 2.75))
    routes_keys = jax.random.split(jax.random.fold_in(key_list[1], 1), TOKENS // TOK_DEV)
    routes_turns = jax.random.permutation(jax.random.fold_in(key_list[1], 3), TOKENS // TOK_DEV)
    routes = jax.vmap(lambda own, number: shared_out(jax.random.fold_in(key_list[1], 2), own, number, TOK_DEV, EXPERTS, TOP, CAP, 2))(routes_keys, routes_turns).reshape((TOKENS, TOP))
    gates = jnp.clip(jnp.exp(math.log(0.5) - 2.3025851 * jax.random.uniform(key_list[2], (TOKENS, TOP), jnp.float32) ** levels(key_list[2], (TOKENS, TOP), ((0, 32),), -0.2, 0.2)), 0.05, 0.5)
    gate_up = noise(key_list[3], (EXPERTS, D, 2 * FFH), D ** -0.5, 0.125, ((0, 8),))
    down_proj = noise(key_list[4], (EXPERTS, FFH, D), FFH ** -0.5, 0.15625, ((0, 8),))
    projection = noise(key_list[5], (D, EMB), D ** -0.5, 0.125)
    matches = jax.vmap(lambda own: jax.random.permutation(own, PATCH))(jax.random.split(key_list[6], PATCHES)).reshape((PATCHES, PATCH)).astype(jnp.int32)
    return dict(tokens=tokens, routes=routes, gates=gates, gate_up=gate_up, down_proj=down_proj, projection=projection, matches=matches)


TEMPER = 0.1
EPSILON = 1e-06

def scores_of(queries, key_rows, matches, coefficient):
    logits = jnp.einsum('pie,pje->pij', queries.astype(jnp.float32), key_rows.astype(jnp.float32)) * coefficient
    totals = jnp.log(lax.optimization_barrier(jnp.sum(jnp.exp(logits), axis=2)))
    target = matches[:, :, None] == jnp.arange(PATCH, dtype=jnp.int32)[None, None, :]
    chosen = lax.optimization_barrier(jnp.sum(jnp.where(target, logits, jnp.zeros_like(logits)), axis=2))
    weights = (jnp.exp(logits - totals[:, :, None]) - target.astype(jnp.float32)).astype(jnp.bfloat16)
    return (totals - chosen, weights)

def reference(tokens, routes, gates, gate_up, down_proj, projection, matches):
    block_count = N_DP * N_EXPERT
    pair_count = TOK_DEV * TOP
    expert_ids = routes.reshape(block_count, pair_count)
    member = (expert_ids[:, :, None] == jnp.arange(EXPERTS, dtype=jnp.int32)[None, None, :]).astype(jnp.int32)
    before = jnp.cumsum(member, axis=1) - member
    position = lax.optimization_barrier(jnp.sum(before * member, axis=2)).astype(jnp.int32)
    block_ids = jnp.broadcast_to(jnp.arange(block_count, dtype=jnp.int32)[:, None], (block_count, pair_count))
    pair_rows = jnp.broadcast_to((jnp.arange(pair_count, dtype=jnp.int32) // TOP)[None, :], (block_count, pair_count))
    row_ids = block_ids * TOK_DEV + pair_rows
    slot_ids = block_ids * CAP + position
    row_table = jnp.full((EXPERTS, block_count * CAP), -1, jnp.int32).at[expert_ids, slot_ids].set(row_ids)
    gate_table = jnp.zeros((EXPERTS, block_count * CAP), jnp.float32).at[expert_ids, slot_ids].set(gates.reshape(block_count, pair_count))

    def forward_slots(joined_w, down_w, row_slots):
        present = row_slots >= 0
        picked = jnp.where(present[:, None], tokens[jnp.maximum(row_slots, 0)], jnp.zeros((), tokens.dtype))
        joined = jnp.dot(picked, joined_w, preferred_element_type=jnp.float32)
        hidden = (jax.nn.silu(joined[:, :FFH]) * joined[:, FFH:]).astype(jnp.bfloat16)
        outputs = jnp.dot(hidden, down_w, preferred_element_type=jnp.float32).astype(jnp.bfloat16)
        return (joined, outputs, present)

    def project_slots(inputs):
        joined, outputs, present = forward_slots(inputs[0], inputs[1], inputs[2])
        return jnp.dot(outputs, projection, preferred_element_type=jnp.float32).astype(jnp.bfloat16)
    projected_table = lax.map(project_slots, (gate_up, down_proj, row_table))
    slot_flat = slot_ids.reshape(TOKENS, TOP)
    mixture = jnp.zeros((TOKENS, EMB), jnp.float32)
    for choice_index in range(TOP):
        picked_proj = projected_table[routes[:, choice_index], slot_flat[:, choice_index]].astype(jnp.float32)
        mixture = mixture + gates[:, choice_index:choice_index + 1] * picked_proj
    embedding = jnp.dot(tokens, projection, preferred_element_type=jnp.float32) + mixture
    inverse = lax.rsqrt(lax.optimization_barrier(jnp.mean(embedding * embedding, axis=1, keepdims=True)) + EPSILON)
    unit_rows = embedding * inverse
    unit_b = unit_rows.astype(jnp.bfloat16)
    coefficient = 1.0 / (EMB * TEMPER)
    partner_index = jnp.bitwise_xor(jnp.arange(N_EXPERT, dtype=jnp.int32), jnp.int32(N_EXPERT // 2))
    patch_shape = (N_DP, N_EXPERT, TOK_DEV // PATCH, PATCH, EMB)
    queries_all = unit_b.reshape(patch_shape)
    queries = queries_all.reshape(PATCHES, PATCH, EMB)
    key_rows = queries_all[:, partner_index].reshape(PATCHES, PATCH, EMB)
    row_loss, weights = scores_of(queries, key_rows, matches, coefficient)
    query_part = jnp.einsum('pij,pje->pie', weights.astype(jnp.float32), key_rows.astype(jnp.float32)) * coefficient
    outgoing = jnp.einsum('pij,pie->pje', weights.astype(jnp.float32), queries.astype(jnp.float32)) * coefficient
    key_part = outgoing.reshape(patch_shape)[:, partner_index].reshape(TOKENS, EMB)
    upstream = query_part.reshape(TOKENS, EMB) + key_part
    embed_grad = inverse * (upstream - unit_rows * lax.optimization_barrier(jnp.mean(upstream * unit_rows, axis=1, keepdims=True)))
    embed_grad_b = embed_grad.astype(jnp.bfloat16)
    direct_grad = jnp.dot(embed_grad_b, projection.T, preferred_element_type=jnp.float32)

    def backward_step(carry, inputs):
        grad_acc, proj_acc = carry
        joined_w, down_w, row_slots, gate_slots = inputs
        joined, outputs, present = forward_slots(joined_w, down_w, row_slots)
        picked_grad = jnp.where(present[:, None], embed_grad_b[jnp.maximum(row_slots, 0)], jnp.zeros((), embed_grad_b.dtype))
        slot_grads = (gate_slots[:, None] * picked_grad.astype(jnp.float32)).astype(jnp.bfloat16)
        output_grads = jnp.dot(slot_grads, projection.T, preferred_element_type=jnp.float32).astype(jnp.bfloat16)
        hidden_grad = jnp.dot(output_grads, down_w.T, preferred_element_type=jnp.float32)
        gate_act = joined[:, :FFH]
        up_act = joined[:, FFH:]
        sigmoid = jax.nn.sigmoid(gate_act)
        joined_grad = jnp.concatenate([hidden_grad * up_act * sigmoid * (1.0 + gate_act * (1.0 - sigmoid)), hidden_grad * gate_act * sigmoid], axis=1).astype(jnp.bfloat16)
        input_grads = jnp.dot(joined_grad, joined_w.T, preferred_element_type=jnp.float32).astype(jnp.bfloat16)
        masked = jnp.where(present[:, None], input_grads.astype(jnp.float32), jnp.zeros((), jnp.float32))
        grad_acc = grad_acc.at[jnp.maximum(row_slots, 0)].add(masked)
        proj_acc = proj_acc + jnp.dot(outputs.T, slot_grads, preferred_element_type=jnp.float32)
        return ((grad_acc, proj_acc), None)
    start_carry = (jnp.zeros((TOKENS, D), jnp.float32), jnp.zeros((D, EMB), jnp.float32))
    final_carry, unused = lax.scan(backward_step, start_carry, (gate_up, down_proj, row_table, gate_table))
    grad_tokens = (direct_grad + final_carry[0]).astype(jnp.bfloat16)
    grad_projection = (jnp.dot(tokens.T, embed_grad_b, preferred_element_type=jnp.float32) + final_carry[1]) * (1.0 / math.sqrt(TOKENS))
    return (grad_tokens, grad_projection, row_loss.reshape(TOKENS))
```

```python
import functools
import math

import jax
import jax.numpy as jnp
from jax import lax
from jax.experimental import pallas as pl
from jax.experimental.pallas import tpu as pltpu
from jax.sharding import PartitionSpec as P

TEMPER = 0.1
EPSILON = 1e-06
CONTRACT_ROWS = (((0,), (0,)), ((), ()))
CONTRACT_COLS = (((1,), (1,)), ((), ()))
PIECES = 2
VMEM_LIMIT = 67043328
MESH = pl.DeviceIdType.MESH


def flip(index, mask):
    bit = 1
    out = index
    while bit <= mask:
        if mask & bit:
            out = out + bit * (1 - 2 * lax.rem(lax.div(index, jnp.int32(bit)), jnp.int32(2)))
        bit *= 2
    return out


def wide_orders(count):
    bits = [1 << b for b in range(1, count.bit_length() - 1)]
    return [bits[p % len(bits):] + bits[:p % len(bits)] for p in range(PIECES)]


def greet(count, dp_count=1):
    me = lax.axis_index("expert")
    barrier = pltpu.get_barrier_semaphore()
    total = 0
    bit = 1
    while bit < count:
        pl.semaphore_signal(barrier, inc=1, device_id={"expert": flip(me, bit)}, device_id_type=MESH)
        total += 1
        bit *= 2
    row = lax.axis_index("dp")
    for offset in range(1, dp_count):
        other = lax.rem(row + offset, jnp.int32(dp_count))
        pl.semaphore_signal(barrier, inc=1, device_id={"dp": other}, device_id_type=MESH)
        total += 1
    pl.semaphore_wait(barrier, total)


def columns(ref, piece, pieces=PIECES):
    width = ref.shape[-1] // pieces
    lead = (slice(None),) * (len(ref.shape) - 1)
    return ref.at[lead + (pl.ds(piece * width, width),)]


def gather_steps(count, own_ref, all_ref, send_sem, recv_sem, pieces=PIECES):
    me = lax.axis_index("expert")
    orders = [order + [1] for order in wide_orders(count)][:pieces]
    copies = {}

    def send(piece, held, bit):
        source = columns(own_ref if held == 0 else all_ref.at[held], piece, pieces)
        target = columns(all_ref.at[held ^ bit], piece, pieces)
        copy = pltpu.make_async_remote_copy(
            src_ref=source,
            dst_ref=target,
            send_sem=send_sem.at[piece, held ^ bit],
            recv_sem=recv_sem.at[piece, held ^ bit],
            device_id={"expert": flip(me, bit)},
            device_id_type=MESH,
        )
        copy.start()
        copies[(piece, held ^ bit)] = copy

    for step in range(len(orders[0])):
        for piece, order in enumerate(orders):
            send(piece, 0, order[step])
    held = [[0] for _ in orders]
    for step in range(len(orders[0])):
        fresh = []
        for piece, order in enumerate(orders):
            arriving = [m ^ order[step] for m in held[piece]]
            fresh.append(arriving)
            held[piece] = held[piece] + arriving
        for slot in range(len(fresh[0])):
            for piece, order in enumerate(orders):
                copies[(piece, fresh[piece][slot])].wait_recv()
                for later in order[step + 1:]:
                    send(piece, fresh[piece][slot], later)
    for copy in copies.values():
        copy.wait_send()


class Scatter:
    def __init__(self, count, block_of, acc_ref, recv_ref, send_sem, recv_sem, cut):
        self.count = count
        self.block_of = block_of
        self.acc_ref = acc_ref
        self.recv_ref = recv_ref
        self.send_sem = send_sem
        self.recv_sem = recv_sem
        self.cut = cut
        self.orders = [[1] + order for order in wide_orders(count)]
        self.held = [list(range(count)) for _ in self.orders]
        self.copies = {}

    def steps(self):
        return len(self.orders[0])

    def value_ref(self, step, piece, block):
        if step == 0:
            return self.cut(self.block_of(block), piece)
        return self.cut(self.acc_ref.at[block // 2], piece)

    def send(self, step, piece):
        me = lax.axis_index("expert")
        bit = self.orders[piece][step]
        for block in sorted(m for m in self.held[piece] if m & bit)[::-1]:
            copy = pltpu.make_async_remote_copy(
                src_ref=self.value_ref(step, piece, block),
                dst_ref=self.cut(self.recv_ref.at[block], piece),
                send_sem=self.send_sem.at[piece, block],
                recv_sem=self.recv_sem.at[piece, block],
                device_id={"expert": flip(me, bit)},
                device_id_type=MESH,
            )
            copy.start()
            self.copies[(piece, block)] = copy

    def fold(self, step, piece):
        bit = self.orders[piece][step]
        kept = [m for m in self.held[piece] if not m & bit]
        last = step == self.steps() - 1
        result = None
        for block in sorted(kept)[::-1]:
            self.copies[(piece, block ^ bit)].wait_recv()
            total = (
                self.value_ref(step, piece, block)[...].astype(jnp.float32)
                + self.cut(self.recv_ref.at[block ^ bit], piece)[...].astype(jnp.float32)
            )
            if last:
                result = total
            else:
                target = self.cut(self.acc_ref.at[block // 2], piece)
                target[...] = total.astype(target.dtype)
        self.held[piece] = kept
        return result

    def finish(self):
        for copy in self.copies.values():
            copy.wait_send()


def gather_kernel(count, own_ref, meta_ref, all_ref, metas_ref, s_send, s_recv, m_send, m_recv, local_sem):
    greet(count)
    keep = pltpu.make_async_copy(own_ref, all_ref.at[0], local_sem.at[0])
    keep_meta = pltpu.make_async_copy(meta_ref, metas_ref.at[0], local_sem.at[1])
    keep_meta.start()
    keep.start()
    gather_steps(count, meta_ref, metas_ref, m_send, m_recv, 1)
    gather_steps(count, own_ref, all_ref, s_send, s_recv)
    keep.wait()
    keep_meta.wait()


def middle_kernel(
    count, coefficient, partial_ref, tokens_ref, projection_ref, mine_ref, match_ref, theirs_ref,
    grads_ref, loss_ref,
    acc_ref, recv_ref, unit_ref, key_ref, grad_ref,
    r_send, r_recv, k_sem, g_send, g_recv, local_sem,
):
    me = lax.axis_index("expert")
    greet(count)
    work = Scatter(count, lambda m: partial_ref.at[m], acc_ref, recv_ref, r_send, r_recv, columns)
    for piece in range(PIECES):
        work.send(0, piece)
    direct = jnp.dot(tokens_ref[...], projection_ref[...], preferred_element_type=jnp.float32)
    parts = []
    for step in range(work.steps()):
        for piece in range(PIECES):
            result = work.fold(step, piece)
            if result is not None:
                parts.append(result)
            else:
                work.send(step + 1, piece)
    embedding = direct + jnp.concatenate(parts, axis=1)
    inverse = lax.rsqrt(jnp.mean(embedding * embedding, axis=1, keepdims=True) + EPSILON)
    unit_rows = embedding * inverse
    unit_b = unit_rows.astype(jnp.bfloat16)
    unit_ref[...] = unit_b
    swap = pltpu.make_async_remote_copy(
        src_ref=unit_ref,
        dst_ref=key_ref,
        send_sem=k_sem.at[0],
        recv_sem=k_sem.at[1],
        device_id={"expert": flip(me, count // 2)},
        device_id_type=MESH,
    )
    swap.start()
    work.finish()
    size = unit_b.shape[0]
    across = lax.broadcasted_iota(jnp.int32, (size, size), 1)
    down = lax.broadcasted_iota(jnp.int32, (size, size), 0)
    target = (match_ref[...] == across).astype(jnp.float32)
    target_theirs = (theirs_ref[...] == down.astype(jnp.float32)).astype(jnp.float32)
    swap.wait()
    keys = key_ref[...]
    logits = lax.dot_general(unit_b, keys, CONTRACT_COLS, preferred_element_type=jnp.float32) * coefficient
    raised = jnp.exp(logits)
    totals = jnp.log(jnp.sum(raised, axis=1, keepdims=True))
    totals_theirs = jnp.log(jnp.sum(raised, axis=0, keepdims=True))
    weights = (jnp.exp(logits - totals) - target).astype(jnp.bfloat16)
    weights_theirs = (jnp.exp(logits - totals_theirs) - target_theirs).astype(jnp.bfloat16)
    upstream = (
        jnp.dot(weights, keys, preferred_element_type=jnp.float32) * coefficient
        + jnp.dot(weights_theirs, keys, preferred_element_type=jnp.float32) * coefficient
    )
    embed_grad = inverse * (upstream - unit_rows * jnp.mean(upstream * unit_rows, axis=1, keepdims=True))
    grad_ref[...] = embed_grad.astype(jnp.bfloat16)
    loss_ref[...] = totals - jnp.sum(logits * target, axis=1, keepdims=True)
    keep = pltpu.make_async_copy(grad_ref, grads_ref.at[0], local_sem.at[0])
    keep.start()
    gather_steps(count, grad_ref, grads_ref, g_send, g_recv)
    keep.wait()


def scatter_kernel(
    count, dp_count, scale, partial_ref, head_ref, grad_ref, projection_ref,
    tokens_out, head_out,
    acc_ref, recv_ref, h_acc, h_recv, z_ref, z_recv,
    r_send, r_recv, h_send, h_rsem, z_send, z_rsem,
):
    me = lax.axis_index("expert")
    row = lax.axis_index("dp")
    greet(count, dp_count)

    def cut_head(ref, piece):
        width = ref.shape[-1] // PIECES
        return ref.at[:, :, pl.ds(piece * width, width)]

    head = Scatter(count, lambda m: head_ref.at[:, flip(me, m)], h_acc, h_recv, h_send, h_rsem, cut_head)
    work = Scatter(count, lambda m: partial_ref.at[m], acc_ref, recv_ref, r_send, r_recv, columns)
    for piece in range(PIECES):
        head.send(0, piece)
    for piece in range(PIECES):
        work.send(0, piece)
    direct = lax.dot_general(
        grad_ref[...], projection_ref[...], CONTRACT_COLS, preferred_element_type=jnp.float32
    )
    tokens_out[...] = direct
    for step in range(head.steps()):
        last = step == head.steps() - 1
        for piece in range(PIECES):
            result = head.fold(step, piece)
            if last:
                target = cut_head(z_ref, piece)
                target[...] = result.astype(z_ref.dtype)
            else:
                head.send(step + 1, piece)
        if last:
            sends = []
            for offset in range(1, dp_count):
                other = lax.rem(row + offset, jnp.int32(dp_count))
                copy = pltpu.make_async_remote_copy(
                    src_ref=z_ref.at[other],
                    dst_ref=z_recv.at[offset],
                    send_sem=z_send.at[offset],
                    recv_sem=z_rsem.at[offset],
                    device_id={"dp": other},
                    device_id_type=MESH,
                )
                copy.start()
                sends.append(copy)
        for piece in range(PIECES):
            result = work.fold(step, piece)
            if last:
                width = tokens_out.shape[1] // PIECES
                cols = pl.ds(piece * width, width)
                tokens_out[:, cols] = tokens_out[:, cols] + result
            else:
                work.send(step + 1, piece)
    total = z_ref[row].astype(jnp.float32)
    for offset, copy in enumerate(sends, 1):
        copy.wait_recv()
        total = total + z_recv[offset].astype(jnp.float32)
    head_out[...] = total * scale
    for copy in sends:
        copy.wait_send()
    head.finish()
    work.finish()


def vmem(count):
    return [pl.BlockSpec(memory_space=pltpu.VMEM)] * count


def params(number):
    return pltpu.CompilerParams(
        collective_id=number, has_side_effects=True, vmem_limit_bytes=VMEM_LIMIT
    )


def dma(*shape):
    return pltpu.SemaphoreType.DMA(shape)


def body(tokens, routes, gates, gate_up, down_proj, projection, matches):
    rows, width = tokens.shape
    top_k = routes.shape[1]
    count = lax.axis_size("expert")
    dp_count = lax.axis_size("dp")
    capacity = rows * top_k * 5 // (count * 4)
    slots = count * capacity
    hidden_width = down_proj.shape[1]
    embed = projection.shape[1]
    me = lax.axis_index("expert")
    bf16 = jnp.bfloat16
    f32 = jnp.float32
    weights_joined = gate_up[0]
    weights_down = down_proj[0]
    meta = jnp.concatenate(
        [routes.astype(f32).T, gates.T, matches.astype(f32)], axis=0
    )
    meta = jnp.pad(meta, ((0, -meta.shape[0] % 8), (0, 0)))
    everyone, metas = pl.pallas_call(
        functools.partial(gather_kernel, count),
        out_shape=(
            jax.ShapeDtypeStruct((count, rows, width), bf16),
            jax.ShapeDtypeStruct((count,) + meta.shape, f32),
        ),
        in_specs=vmem(2),
        out_specs=tuple(vmem(2)),
        scratch_shapes=[
            dma(PIECES, count), dma(PIECES, count), dma(1, count), dma(1, count), dma(2),
        ],
        compiler_params=params(0),
        name="gather_tokens",
    )(tokens, meta)
    chosen = metas[:, :top_k, :] == me.astype(f32)
    member = jnp.any(chosen, axis=1)
    gate_rows = jnp.sum(jnp.where(chosen, metas[:, top_k:2 * top_k, :], 0.0), axis=1)
    earlier = (jnp.arange(rows)[:, None] < jnp.arange(rows)[None, :]).astype(bf16)
    position = jnp.dot(member.astype(bf16), earlier, preferred_element_type=f32)
    slot_range = jnp.arange(capacity, dtype=jnp.int32).astype(f32)
    chooser = (
        member[:, None, :] & (position[:, None, :] == slot_range[None, :, None])
    ).astype(bf16)
    flat_input = jnp.einsum("scr,srd->scd", chooser, everyone, preferred_element_type=f32)
    flat_input = flat_input.astype(bf16).reshape(slots, width)
    joined = jnp.dot(flat_input, weights_joined, preferred_element_type=f32)
    hidden = (jax.nn.silu(joined[:, :hidden_width]) * joined[:, hidden_width:]).astype(bf16)
    outputs = jnp.dot(hidden, weights_down, preferred_element_type=f32).astype(bf16)
    projected = jnp.dot(outputs, projection, preferred_element_type=f32).astype(bf16)
    spread = jnp.einsum(
        "scr,sce->sre", chooser, projected.reshape(count, capacity, embed),
        preferred_element_type=f32,
    )
    partial = (gate_rows[:, :, None] * spread).astype(bf16)
    coefficient = 1.0 / (embed * TEMPER)
    theirs = metas[count // 2, 2 * top_k:2 * top_k + 1, :]
    half = max(1, count // 2)
    all_grads, loss = pl.pallas_call(
        functools.partial(middle_kernel, count, coefficient),
        out_shape=(
            jax.ShapeDtypeStruct((count, rows, embed), bf16),
            jax.ShapeDtypeStruct((rows, 1), f32),
        ),
        in_specs=vmem(6),
        out_specs=tuple(vmem(2)),
        scratch_shapes=[
            pltpu.VMEM((half, rows, embed), bf16),
            pltpu.VMEM((count, rows, embed), bf16),
            pltpu.VMEM((rows, embed), bf16),
            pltpu.VMEM((rows, embed), bf16),
            pltpu.VMEM((rows, embed), bf16),
            dma(PIECES, count), dma(PIECES, count), dma(2),
            dma(PIECES, count), dma(PIECES, count), dma(1),
        ],
        compiler_params=params(1),
        name="contrast",
    )(partial, tokens, projection, matches, matches.reshape(rows, 1), theirs)
    embed_grad = all_grads[0]
    gated = (gate_rows[:, :, None] * all_grads.astype(f32)).astype(bf16)
    slot_grads = jnp.einsum("scr,sre->sce", chooser, gated, preferred_element_type=f32)
    slot_grads = slot_grads.astype(bf16).reshape(slots, embed)
    output_grads = lax.dot_general(
        slot_grads, projection, CONTRACT_COLS, preferred_element_type=f32
    ).astype(bf16)
    hidden_grad = lax.dot_general(
        output_grads, weights_down, CONTRACT_COLS, preferred_element_type=f32
    )
    gate_act = joined[:, :hidden_width]
    up_act = joined[:, hidden_width:]
    sigmoid = jax.nn.sigmoid(gate_act)
    joined_grad = jnp.concatenate(
        [
            hidden_grad * up_act * sigmoid * (1.0 + gate_act * (1.0 - sigmoid)),
            hidden_grad * gate_act * sigmoid,
        ],
        axis=1,
    ).astype(bf16)
    input_grads = lax.dot_general(
        joined_grad, weights_joined, CONTRACT_COLS, preferred_element_type=f32
    ).astype(bf16)
    back = jnp.einsum(
        "scr,scd->srd", chooser, input_grads.reshape(count, capacity, width),
        preferred_element_type=f32,
    ).astype(bf16)
    head = lax.dot_general(tokens, embed_grad, CONTRACT_ROWS, preferred_element_type=f32)
    head = head + lax.dot_general(outputs, slot_grads, CONTRACT_ROWS, preferred_element_type=f32)
    share = width // (count * dp_count)
    head = head.astype(bf16).reshape(dp_count, count, share, embed)
    scale = 1.0 / math.sqrt(rows * count * dp_count)
    grad_tokens, grad_projection = pl.pallas_call(
        functools.partial(scatter_kernel, count, dp_count, scale),
        out_shape=(
            jax.ShapeDtypeStruct((rows, width), f32),
            jax.ShapeDtypeStruct((share, embed), f32),
        ),
        in_specs=vmem(4),
        out_specs=tuple(vmem(2)),
        scratch_shapes=[
            pltpu.VMEM((half, rows, width), bf16),
            pltpu.VMEM((count, rows, width), bf16),
            pltpu.VMEM((half, dp_count, share, embed), bf16),
            pltpu.VMEM((count, dp_count, share, embed), bf16),
            pltpu.VMEM((dp_count, share, embed), bf16),
            pltpu.VMEM((dp_count, share, embed), bf16),
            dma(PIECES, count), dma(PIECES, count),
            dma(PIECES, count), dma(PIECES, count),
            dma(dp_count), dma(dp_count),
        ],
        compiler_params=params(2),
        name="scatter_grads",
    )(back, head, embed_grad, projection)
    return (grad_tokens.astype(bf16), grad_projection, loss.reshape(rows))


def solution(mesh):
    placed = (
        P(("dp", "expert"), None),
        P(("dp", "expert"), None),
        P(("dp", "expert"), None),
        P("expert", None, None),
        P("expert", None, None),
        P(),
        P(("dp", "expert"), None),
    )
    return jax.shard_map(
        body,
        mesh=mesh,
        in_specs=placed,
        out_specs=(P(("dp", "expert"), None), P(("dp", "expert"), None), P(("dp", "expert"))),
        check_vma=False,
    )
```

```python
import functools
import math

import jax
import jax.numpy as jnp
from jax import lax
from jax.experimental import pallas as pl
from jax.experimental.pallas import tpu as pltpu
from jax.sharding import PartitionSpec as P

TEMPER = 0.1
EPSILON = 1e-06
CONTRACT_ROWS = (((0,), (0,)), ((), ()))
CONTRACT_COLS = (((1,), (1,)), ((), ()))
PIECES = 2
WORK_PIECES = 4
VMEM_LIMIT = 67043328
MESH = pl.DeviceIdType.MESH


def flip(index, mask):
    bit = 1
    out = index
    while bit <= mask:
        if mask & bit:
            out = out + bit * (1 - 2 * lax.rem(lax.div(index, jnp.int32(bit)), jnp.int32(2)))
        bit *= 2
    return out


def wide_orders(count, pieces=PIECES):
    bits = [1 << b for b in range(1, count.bit_length() - 1)]
    return [bits[p % len(bits):] + bits[:p % len(bits)] for p in range(pieces)]


def greet(count, dp_count=1):
    me = lax.axis_index("expert")
    barrier = pltpu.get_barrier_semaphore()
    total = 0
    bit = 1
    while bit < count:
        pl.semaphore_signal(barrier, inc=1, device_id={"expert": flip(me, bit)}, device_id_type=MESH)
        total += 1
        bit *= 2
    row = lax.axis_index("dp")
    for offset in range(1, dp_count):
        other = lax.rem(row + offset, jnp.int32(dp_count))
        pl.semaphore_signal(barrier, inc=1, device_id={"dp": other}, device_id_type=MESH)
        total += 1
    pl.semaphore_wait(barrier, total)


def columns(ref, piece, pieces=PIECES):
    width = ref.shape[-1] // pieces
    lead = (slice(None),) * (len(ref.shape) - 1)
    return ref.at[lead + (pl.ds(piece * width, width),)]


def gather_steps(count, own_ref, all_ref, send_sem, recv_sem, pieces=PIECES):
    me = lax.axis_index("expert")
    orders = [order + [1] for order in wide_orders(count, pieces)]
    copies = {}

    def send(piece, held, bit):
        source = columns(own_ref if held == 0 else all_ref.at[held], piece, pieces)
        target = columns(all_ref.at[held ^ bit], piece, pieces)
        copy = pltpu.make_async_remote_copy(
            src_ref=source,
            dst_ref=target,
            send_sem=send_sem.at[piece, held ^ bit],
            recv_sem=recv_sem.at[piece, held ^ bit],
            device_id={"expert": flip(me, bit)},
            device_id_type=MESH,
        )
        copy.start()
        copies[(piece, held ^ bit)] = copy

    for step in range(len(orders[0])):
        for piece, order in enumerate(orders):
            send(piece, 0, order[step])
    held = [[0] for _ in orders]
    for step in range(len(orders[0])):
        fresh = []
        for piece, order in enumerate(orders):
            arriving = [m ^ order[step] for m in held[piece]]
            fresh.append(arriving)
            held[piece] = held[piece] + arriving
        for slot in range(len(fresh[0])):
            for piece, order in enumerate(orders):
                copies[(piece, fresh[piece][slot])].wait_recv()
                for later in order[step + 1:]:
                    send(piece, fresh[piece][slot], later)
    for copy in copies.values():
        copy.wait_send()


class Scatter:
    def __init__(self, count, block_of, acc_of, recv_ref, send_sem, recv_sem, cut, pieces=PIECES):
        self.count = count
        self.block_of = block_of
        self.acc_of = acc_of
        self.recv_ref = recv_ref
        self.send_sem = send_sem
        self.recv_sem = recv_sem
        self.cut = cut
        self.orders = [[1] + order for order in wide_orders(count, pieces)]
        self.held = [list(range(count)) for _ in self.orders]
        self.copies = {}

    def steps(self):
        return len(self.orders[0])

    def value_ref(self, step, piece, block):
        if step == 0:
            return self.cut(self.block_of(block), piece)
        return self.cut(self.acc_of(block), piece)

    def send(self, step, piece):
        me = lax.axis_index("expert")
        bit = self.orders[piece][step]
        for block in sorted(m for m in self.held[piece] if m & bit)[::-1]:
            copy = pltpu.make_async_remote_copy(
                src_ref=self.value_ref(step, piece, block),
                dst_ref=self.cut(self.recv_ref.at[block], piece),
                send_sem=self.send_sem.at[piece, block],
                recv_sem=self.recv_sem.at[piece, block],
                device_id={"expert": flip(me, bit)},
                device_id_type=MESH,
            )
            copy.start()
            self.copies[(piece, block)] = copy

    def fold(self, step, piece):
        bit = self.orders[piece][step]
        kept = [m for m in self.held[piece] if not m & bit]
        last = step == self.steps() - 1
        result = None
        for block in sorted(kept)[::-1]:
            self.copies[(piece, block ^ bit)].wait_recv()
            total = (
                self.value_ref(step, piece, block)[...].astype(jnp.float32)
                + self.cut(self.recv_ref.at[block ^ bit], piece)[...].astype(jnp.float32)
            )
            if last:
                result = total
            else:
                target = self.cut(self.acc_of(block), piece)
                target[...] = total.astype(target.dtype)
        self.held[piece] = kept
        return result

    def finish(self):
        for copy in self.copies.values():
            copy.wait_send()


def gather_kernel(count, own_ref, meta_ref, all_ref, metas_ref, s_send, s_recv, m_send, m_recv, local_sem):
    greet(count)
    keep = pltpu.make_async_copy(own_ref, all_ref.at[0], local_sem.at[0])
    keep_meta = pltpu.make_async_copy(meta_ref, metas_ref.at[0], local_sem.at[1])
    keep_meta.start()
    keep.start()
    gather_steps(count, meta_ref, metas_ref, m_send, m_recv, 1)
    gather_steps(count, own_ref, all_ref, s_send, s_recv)
    keep.wait()
    keep_meta.wait()


def middle_kernel(
    count, coefficient, match_row, partial_ref, tokens_ref, projection_ref, metas_ref,
    grads_ref, loss_ref,
    acc_ref, recv_ref, unit_ref, key_ref, grad_ref,
    r_send, r_recv, k_sem, g_send, g_recv, local_sem,
):
    me = lax.axis_index("expert")
    greet(count)
    work = Scatter(
        count, lambda m: partial_ref.at[m], lambda m: acc_ref.at[m // 2], recv_ref, r_send, r_recv, columns
    )
    for piece in range(PIECES):
        work.send(0, piece)
    direct = jnp.dot(tokens_ref[...], projection_ref[...], preferred_element_type=jnp.float32)
    parts = []
    for step in range(work.steps()):
        for piece in range(PIECES):
            result = work.fold(step, piece)
            if result is not None:
                parts.append(result)
            else:
                work.send(step + 1, piece)
    embedding = direct + jnp.concatenate(parts, axis=1)
    inverse = lax.rsqrt(jnp.mean(embedding * embedding, axis=1, keepdims=True) + EPSILON)
    unit_rows = embedding * inverse
    unit_b = unit_rows.astype(jnp.bfloat16)
    unit_ref[...] = unit_b
    swap = pltpu.make_async_remote_copy(
        src_ref=unit_ref,
        dst_ref=key_ref,
        send_sem=k_sem.at[0],
        recv_sem=k_sem.at[1],
        device_id={"expert": flip(me, count // 2)},
        device_id_type=MESH,
    )
    swap.start()
    work.finish()
    size = unit_b.shape[0]
    across = lax.broadcasted_iota(jnp.int32, (size, size), 1)
    down = lax.broadcasted_iota(jnp.int32, (size, size), 0)
    diagonal = across == down
    mine = metas_ref[0, match_row:match_row + 1, :]
    theirs = metas_ref[count // 2, match_row:match_row + 1, :]
    column = jnp.sum(jnp.where(diagonal, mine, 0.0), axis=1, keepdims=True)
    target = (column == across.astype(jnp.float32)).astype(jnp.float32)
    target_theirs = (theirs == down.astype(jnp.float32)).astype(jnp.float32)
    swap.wait()
    keys = key_ref[...]
    logits = lax.dot_general(unit_b, keys, CONTRACT_COLS, preferred_element_type=jnp.float32) * coefficient
    raised = jnp.exp(logits)
    totals = jnp.log(jnp.sum(raised, axis=1, keepdims=True))
    totals_theirs = jnp.log(jnp.sum(raised, axis=0, keepdims=True))
    weights = (jnp.exp(logits - totals) - target).astype(jnp.bfloat16)
    weights_theirs = (jnp.exp(logits - totals_theirs) - target_theirs).astype(jnp.bfloat16)
    upstream = (
        jnp.dot(weights, keys, preferred_element_type=jnp.float32) * coefficient
        + jnp.dot(weights_theirs, keys, preferred_element_type=jnp.float32) * coefficient
    )
    embed_grad = inverse * (upstream - unit_rows * jnp.mean(upstream * unit_rows, axis=1, keepdims=True))
    grad_ref[...] = embed_grad.astype(jnp.bfloat16)
    keep = pltpu.make_async_copy(grad_ref, grads_ref.at[0], local_sem.at[0])
    keep.start()
    loss = totals - jnp.sum(logits * target, axis=1, keepdims=True)
    loss_ref[...] = jnp.sum(jnp.where(diagonal, loss, 0.0), axis=0, keepdims=True)
    gather_steps(count, grad_ref, grads_ref, g_send, g_recv)
    keep.wait()


def scatter_kernel(
    count, dp_count, scale, joined_ref, spread_ref, weights_ref, head_ref, grads_ref, projection_ref,
    tokens_out, head_out,
    back_ref, recv_ref, tile_ref, direct_ref, h_acc, h_recv, z_ref, z_recv,
    tile_sem, r_send, r_recv, h_send, h_rsem, z_send, z_rsem,
):
    me = lax.axis_index("expert")
    row = lax.axis_index("dp")
    tile = tile_ref.shape[1]
    tiles = weights_ref.shape[0] // tile
    capacity = spread_ref.shape[2]

    def load(number):
        return pltpu.make_async_copy(
            weights_ref.at[pl.ds(number * tile, tile)], tile_ref.at[number % 2], tile_sem.at[number % 2]
        )

    load(0).start()
    greet(count, dp_count)

    def cut_head(ref, piece):
        width = ref.shape[-1] // PIECES
        return ref.at[:, :, pl.ds(piece * width, width)]

    def cut_work(ref, piece):
        return columns(ref, piece, WORK_PIECES)

    head = Scatter(
        count, lambda m: head_ref.at[:, flip(me, m)], lambda m: h_acc.at[m // 2], h_recv, h_send, h_rsem, cut_head
    )
    work = Scatter(
        count, lambda m: back_ref.at[m], lambda m: back_ref.at[m], recv_ref, r_send, r_recv, cut_work, WORK_PIECES
    )
    for piece in range(PIECES):
        head.send(0, piece)
    sends = []

    def head_step(step):
        last = step == head.steps() - 1
        for piece in range(PIECES):
            result = head.fold(step, piece)
            if last:
                target = cut_head(z_ref, piece)
                target[...] = result.astype(z_ref.dtype)
            else:
                head.send(step + 1, piece)
        if last:
            for offset in range(1, dp_count):
                other = lax.rem(row + offset, jnp.int32(dp_count))
                copy = pltpu.make_async_remote_copy(
                    src_ref=z_ref.at[other],
                    dst_ref=z_recv.at[offset],
                    send_sem=z_send.at[offset],
                    recv_sem=z_rsem.at[offset],
                    device_id={"dp": other},
                    device_id_type=MESH,
                )
                copy.start()
                sends.append(copy)

    def work_step(step, piece):
        result = work.fold(step, piece)
        if step == work.steps() - 1:
            width = tokens_out.shape[1] // WORK_PIECES
            cols = pl.ds(piece * width, width)
            tokens_out[:, cols] = (direct_ref[:, cols] + result).astype(tokens_out.dtype)
        else:
            work.send(step + 1, piece)

    for turn in range(WORK_PIECES + work.steps()):
        if turn < WORK_PIECES:
            for number in range(turn * tiles // WORK_PIECES, (turn + 1) * tiles // WORK_PIECES):
                load(number).wait()
                if number + 1 < tiles:
                    load(number + 1).start()
                cols = pl.ds(number * tile, tile)
                grads = lax.dot_general(
                    joined_ref[...], tile_ref[number % 2], CONTRACT_COLS, preferred_element_type=jnp.float32
                ).astype(jnp.bfloat16)
                for block in range(count):
                    back_ref[block, :, cols] = jnp.dot(
                        spread_ref[block], grads[block * capacity:(block + 1) * capacity],
                        preferred_element_type=jnp.float32,
                    ).astype(jnp.bfloat16)
                direct_ref[:, cols] = lax.dot_general(
                    grads_ref[0], projection_ref[cols, :], CONTRACT_COLS, preferred_element_type=jnp.float32
                )
            work.send(0, turn)
        for step in reversed(range(work.steps())):
            piece = turn - 1 - step
            if 0 <= piece < WORK_PIECES:
                work_step(step, piece)
        if turn < head.steps():
            head_step(turn)
    total = z_ref[row].astype(jnp.float32)
    for offset, copy in enumerate(sends, 1):
        copy.wait_recv()
        total = total + z_recv[offset].astype(jnp.float32)
    head_out[...] = total * scale
    for copy in sends:
        copy.wait_send()
    head.finish()
    work.finish()


def vmem(count):
    return [pl.BlockSpec(memory_space=pltpu.VMEM)] * count


def params(number):
    return pltpu.CompilerParams(
        collective_id=number, has_side_effects=True, vmem_limit_bytes=VMEM_LIMIT
    )


def dma(*shape):
    return pltpu.SemaphoreType.DMA(shape)


def body(tokens, routes, gates, gate_up, down_proj, projection, matches):
    rows, width = tokens.shape
    top_k = routes.shape[1]
    count = lax.axis_size("expert")
    dp_count = lax.axis_size("dp")
    capacity = -(-(rows * top_k * 5 // (count * 4)) // 16) * 16
    slots = count * capacity
    hidden_width = down_proj.shape[1]
    embed = projection.shape[1]
    me = lax.axis_index("expert")
    bf16 = jnp.bfloat16
    f32 = jnp.float32
    weights_joined = gate_up[0]
    weights_down = down_proj[0]
    meta = jnp.concatenate(
        [routes.astype(f32).T, gates.T, matches.astype(f32)], axis=0
    )
    meta = jnp.pad(meta, ((0, -meta.shape[0] % 8), (0, 0)))
    everyone, metas = pl.pallas_call(
        functools.partial(gather_kernel, count),
        out_shape=(
            jax.ShapeDtypeStruct((count, rows, width), bf16),
            jax.ShapeDtypeStruct((count,) + meta.shape, f32),
        ),
        in_specs=vmem(2),
        out_specs=tuple(vmem(2)),
        scratch_shapes=[
            dma(PIECES, count), dma(PIECES, count), dma(1, count), dma(1, count), dma(2),
        ],
        compiler_params=params(0),
        name="gather_tokens",
    )(tokens, meta)
    chosen = metas[:, :top_k, :] == me.astype(f32)
    member = jnp.any(chosen, axis=1)
    gate_rows = jnp.sum(jnp.where(chosen, metas[:, top_k:2 * top_k, :], 0.0), axis=1)
    earlier = (jnp.arange(rows)[:, None] < jnp.arange(rows)[None, :]).astype(bf16)
    position = jnp.dot(member.astype(bf16), earlier, preferred_element_type=f32)
    slot_range = jnp.arange(capacity, dtype=jnp.int32).astype(f32)
    chooser = (
        member[:, None, :] & (position[:, None, :] == slot_range[None, :, None])
    ).astype(bf16)
    flat_input = jnp.einsum("scr,srd->scd", chooser, everyone, preferred_element_type=f32)
    flat_input = flat_input.astype(bf16).reshape(slots, width)
    joined = jnp.dot(flat_input, weights_joined, preferred_element_type=f32)
    hidden = (jax.nn.silu(joined[:, :hidden_width]) * joined[:, hidden_width:]).astype(bf16)
    outputs = jnp.dot(hidden, weights_down, preferred_element_type=f32).astype(bf16)
    projected = jnp.dot(outputs, projection, preferred_element_type=f32).astype(bf16)
    spread = jnp.einsum(
        "scr,sce->sre", chooser, projected.reshape(count, capacity, embed),
        preferred_element_type=f32,
    )
    partial = (gate_rows[:, :, None] * spread).astype(bf16)
    coefficient = 1.0 / (embed * TEMPER)
    half = max(1, count // 2)
    all_grads, loss = pl.pallas_call(
        functools.partial(middle_kernel, count, coefficient, 2 * top_k),
        out_shape=(
            jax.ShapeDtypeStruct((count, rows, embed), bf16),
            jax.ShapeDtypeStruct((1, rows), f32),
        ),
        in_specs=vmem(4),
        out_specs=tuple(vmem(2)),
        scratch_shapes=[
            pltpu.VMEM((half, rows, embed), bf16),
            pltpu.VMEM((count, rows, embed), bf16),
            pltpu.VMEM((rows, embed), bf16),
            pltpu.VMEM((rows, embed), bf16),
            pltpu.VMEM((rows, embed), bf16),
            dma(PIECES, count), dma(PIECES, count), dma(2),
            dma(PIECES, count), dma(PIECES, count), dma(1),
        ],
        compiler_params=params(1),
        name="contrast",
    )(partial, tokens, projection, metas)
    embed_grad = all_grads[0]
    gated = (gate_rows[:, :, None] * all_grads.astype(f32)).astype(bf16)
    slot_grads = jnp.einsum("scr,sre->sce", chooser, gated, preferred_element_type=f32)
    slot_grads = slot_grads.astype(bf16).reshape(slots, embed)
    output_grads = lax.dot_general(
        slot_grads, projection, CONTRACT_COLS, preferred_element_type=f32
    ).astype(bf16)
    hidden_grad = lax.dot_general(
        output_grads, weights_down, CONTRACT_COLS, preferred_element_type=f32
    )
    gate_act = joined[:, :hidden_width]
    up_act = joined[:, hidden_width:]
    sigmoid = jax.nn.sigmoid(gate_act)
    joined_grad = jnp.concatenate(
        [
            hidden_grad * up_act * sigmoid * (1.0 + gate_act * (1.0 - sigmoid)),
            hidden_grad * gate_act * sigmoid,
        ],
        axis=1,
    ).astype(bf16)
    spread_back = chooser.transpose(0, 2, 1)
    head = lax.dot_general(tokens, embed_grad, CONTRACT_ROWS, preferred_element_type=f32)
    head = head + lax.dot_general(outputs, slot_grads, CONTRACT_ROWS, preferred_element_type=f32)
    share = width // (count * dp_count)
    head = head.astype(bf16).reshape(dp_count, count, share, embed)
    scale = 1.0 / math.sqrt(rows * count * dp_count)
    grad_tokens, grad_projection = pl.pallas_call(
        functools.partial(scatter_kernel, count, dp_count, scale),
        out_shape=(
            jax.ShapeDtypeStruct((rows, width), bf16),
            jax.ShapeDtypeStruct((share, embed), f32),
        ),
        in_specs=vmem(2) + [pl.BlockSpec(memory_space=pl.ANY)] + vmem(3),
        out_specs=tuple(vmem(2)),
        scratch_shapes=[
            pltpu.VMEM((count, rows, width), bf16),
            pltpu.VMEM((count, rows, width), bf16),
            pltpu.VMEM((2, width // 8, 2 * hidden_width), bf16),
            pltpu.VMEM((rows, width), f32),
            pltpu.VMEM((half, dp_count, share, embed), bf16),
            pltpu.VMEM((count, dp_count, share, embed), bf16),
            pltpu.VMEM((dp_count, share, embed), bf16),
            pltpu.VMEM((dp_count, share, embed), bf16),
            dma(2),
            dma(WORK_PIECES, count), dma(WORK_PIECES, count),
            dma(PIECES, count), dma(PIECES, count),
            dma(dp_count), dma(dp_count),
        ],
        compiler_params=params(2),
        name="scatter_grads",
    )(joined_grad, spread_back, weights_joined, head, all_grads, projection)
    return (grad_tokens, grad_projection, loss.reshape(rows))


def solution(mesh):
    placed = (
        P(("dp", "expert"), None),
        P(("dp", "expert"), None),
        P(("dp", "expert"), None),
        P("expert", None, None),
        P("expert", None, None),
        P(),
        P(("dp", "expert"), None),
    )
    return jax.shard_map(
        body,
        mesh=mesh,
        in_specs=placed,
        out_specs=(P(("dp", "expert"), None), P(("dp", "expert"), None), P(("dp", "expert"))),
        check_vma=False,
    )
```

```python
import functools
import math

import jax
import jax.numpy as jnp
from jax import lax
from jax.experimental import pallas as pl
from jax.experimental.pallas import tpu as pltpu
from jax.sharding import PartitionSpec as P

TEMPER = 0.1
EPSILON = 1e-06
CONTRACT_ROWS = (((0,), (0,)), ((), ()))
CONTRACT_COLS = (((1,), (1,)), ((), ()))
PIECES = 2
WORK_PIECES = 4
VMEM_LIMIT = 67043328
MESH = pl.DeviceIdType.MESH


def flip(index, mask):
    bit = 1
    out = index
    while bit <= mask:
        if mask & bit:
            out = out + bit * (1 - 2 * lax.rem(lax.div(index, jnp.int32(bit)), jnp.int32(2)))
        bit *= 2
    return out


def wide_orders(count, pieces=PIECES):
    bits = [1 << b for b in range(1, count.bit_length() - 1)]
    return [bits[p % len(bits):] + bits[:p % len(bits)] for p in range(pieces)]


def greet(count, dp_count=1):
    me = lax.axis_index("expert")
    barrier = pltpu.get_barrier_semaphore()
    total = 0
    bit = 1
    while bit < count:
        pl.semaphore_signal(barrier, inc=1, device_id={"expert": flip(me, bit)}, device_id_type=MESH)
        total += 1
        bit *= 2
    row = lax.axis_index("dp")
    for offset in range(1, dp_count):
        other = lax.rem(row + offset, jnp.int32(dp_count))
        pl.semaphore_signal(barrier, inc=1, device_id={"dp": other}, device_id_type=MESH)
        total += 1
    pl.semaphore_wait(barrier, total)


def columns(ref, piece, pieces=PIECES):
    width = ref.shape[-1] // pieces
    lead = (slice(None),) * (len(ref.shape) - 1)
    return ref.at[lead + (pl.ds(piece * width, width),)]


def gather_steps(count, own_ref, all_ref, send_sem, recv_sem, pieces=PIECES):
    me = lax.axis_index("expert")
    orders = [order + [1] for order in wide_orders(count, pieces)]
    copies = {}

    def send(piece, held, bit):
        source = columns(own_ref if held == 0 else all_ref.at[held], piece, pieces)
        target = columns(all_ref.at[held ^ bit], piece, pieces)
        copy = pltpu.make_async_remote_copy(
            src_ref=source,
            dst_ref=target,
            send_sem=send_sem.at[piece, held ^ bit],
            recv_sem=recv_sem.at[piece, held ^ bit],
            device_id={"expert": flip(me, bit)},
            device_id_type=MESH,
        )
        copy.start()
        copies[(piece, held ^ bit)] = copy

    for step in range(len(orders[0])):
        for piece, order in enumerate(orders):
            send(piece, 0, order[step])
    held = [[0] for _ in orders]
    for step in range(len(orders[0])):
        fresh = []
        for piece, order in enumerate(orders):
            arriving = [m ^ order[step] for m in held[piece]]
            fresh.append(arriving)
            held[piece] = held[piece] + arriving
        for slot in range(len(fresh[0])):
            for piece, order in enumerate(orders):
                copies[(piece, fresh[piece][slot])].wait_recv()
                for later in order[step + 1:]:
                    send(piece, fresh[piece][slot], later)
    for copy in copies.values():
        copy.wait_send()


class Scatter:
    def __init__(self, count, block_of, acc_of, recv_ref, send_sem, recv_sem, cut, pieces=PIECES):
        self.count = count
        self.block_of = block_of
        self.acc_of = acc_of
        self.recv_ref = recv_ref
        self.send_sem = send_sem
        self.recv_sem = recv_sem
        self.cut = cut
        self.orders = [[1] + order for order in wide_orders(count, pieces)]
        self.held = [list(range(count)) for _ in self.orders]
        self.copies = {}

    def steps(self):
        return len(self.orders[0])

    def value_ref(self, step, piece, block):
        if step == 0:
            return self.cut(self.block_of(block), piece)
        return self.cut(self.acc_of(block), piece)

    def send(self, step, piece):
        me = lax.axis_index("expert")
        bit = self.orders[piece][step]
        for block in sorted(m for m in self.held[piece] if m & bit)[::-1]:
            copy = pltpu.make_async_remote_copy(
                src_ref=self.value_ref(step, piece, block),
                dst_ref=self.cut(self.recv_ref.at[block], piece),
                send_sem=self.send_sem.at[piece, block],
                recv_sem=self.recv_sem.at[piece, block],
                device_id={"expert": flip(me, bit)},
                device_id_type=MESH,
            )
            copy.start()
            self.copies[(piece, block)] = copy

    def fold(self, step, piece):
        bit = self.orders[piece][step]
        kept = [m for m in self.held[piece] if not m & bit]
        last = step == self.steps() - 1
        result = None
        for block in sorted(kept)[::-1]:
            self.copies[(piece, block ^ bit)].wait_recv()
            total = (
                self.value_ref(step, piece, block)[...].astype(jnp.float32)
                + self.cut(self.recv_ref.at[block ^ bit], piece)[...].astype(jnp.float32)
            )
            if last:
                result = total
            else:
                target = self.cut(self.acc_of(block), piece)
                target[...] = total.astype(target.dtype)
        self.held[piece] = kept
        return result

    def finish(self):
        for copy in self.copies.values():
            copy.wait_send()


def gather_kernel(count, own_ref, meta_ref, all_ref, metas_ref, s_send, s_recv, m_send, m_recv, local_sem):
    greet(count)
    keep = pltpu.make_async_copy(own_ref, all_ref.at[0], local_sem.at[0])
    keep_meta = pltpu.make_async_copy(meta_ref, metas_ref.at[0], local_sem.at[1])
    keep_meta.start()
    keep.start()
    gather_steps(count, meta_ref, metas_ref, m_send, m_recv, 1)
    gather_steps(count, own_ref, all_ref, s_send, s_recv)
    keep.wait()
    keep_meta.wait()


def middle_kernel(
    count, coefficient, match_row, partial_ref, tokens_ref, projection_ref, metas_ref,
    grads_ref, loss_ref,
    acc_ref, recv_ref, unit_ref, key_ref, grad_ref,
    r_send, r_recv, k_sem, g_send, g_recv, local_sem,
):
    me = lax.axis_index("expert")
    greet(count)
    work = Scatter(
        count, lambda m: partial_ref.at[m], lambda m: acc_ref.at[m // 2], recv_ref, r_send, r_recv, columns
    )
    for piece in range(PIECES):
        work.send(0, piece)
    parts = []
    for step in range(work.steps()):
        for piece in range(PIECES):
            result = work.fold(step, piece)
            if result is not None:
                parts.append(result)
            else:
                work.send(step + 1, piece)
        if step == 0:
            direct = jnp.dot(tokens_ref[...], projection_ref[...], preferred_element_type=jnp.float32)
    embedding = direct + jnp.concatenate(parts, axis=1)
    inverse = lax.rsqrt(jnp.mean(embedding * embedding, axis=1, keepdims=True) + EPSILON)
    unit_rows = embedding * inverse
    unit_b = unit_rows.astype(jnp.bfloat16)
    unit_ref[...] = unit_b
    swap = pltpu.make_async_remote_copy(
        src_ref=unit_ref,
        dst_ref=key_ref,
        send_sem=k_sem.at[0],
        recv_sem=k_sem.at[1],
        device_id={"expert": flip(me, count // 2)},
        device_id_type=MESH,
    )
    swap.start()
    work.finish()
    size = unit_b.shape[0]
    across = lax.broadcasted_iota(jnp.int32, (size, size), 1)
    down = lax.broadcasted_iota(jnp.int32, (size, size), 0)
    diagonal = across == down
    mine = metas_ref[0, match_row:match_row + 1, :]
    theirs = metas_ref[count // 2, match_row:match_row + 1, :]
    column = jnp.sum(jnp.where(diagonal, mine, 0.0), axis=1, keepdims=True)
    target = (column == across.astype(jnp.float32)).astype(jnp.float32)
    target_theirs = (theirs == down.astype(jnp.float32)).astype(jnp.float32)
    swap.wait()
    keys = key_ref[...]
    logits = lax.dot_general(unit_b, keys, CONTRACT_COLS, preferred_element_type=jnp.float32) * coefficient
    raised = jnp.exp(logits)
    totals = jnp.log(jnp.sum(raised, axis=1, keepdims=True))
    totals_theirs = jnp.log(jnp.sum(raised, axis=0, keepdims=True))
    weights = (jnp.exp(logits - totals) - target).astype(jnp.bfloat16)
    weights_theirs = (jnp.exp(logits - totals_theirs) - target_theirs).astype(jnp.bfloat16)
    upstream = (
        jnp.dot(weights, keys, preferred_element_type=jnp.float32) * coefficient
        + jnp.dot(weights_theirs, keys, preferred_element_type=jnp.float32) * coefficient
    )
    embed_grad = inverse * (upstream - unit_rows * jnp.mean(upstream * unit_rows, axis=1, keepdims=True))
    grad_ref[...] = embed_grad.astype(jnp.bfloat16)
    keep = pltpu.make_async_copy(grad_ref, grads_ref.at[0], local_sem.at[0])
    keep.start()
    loss = totals - jnp.sum(logits * target, axis=1, keepdims=True)
    loss_ref[...] = jnp.sum(jnp.where(diagonal, loss, 0.0), axis=0, keepdims=True)
    gather_steps(count, grad_ref, grads_ref, g_send, g_recv)
    keep.wait()


def scatter_kernel(
    count, dp_count, scale, partial_ref, head_ref, grads_ref, projection_ref,
    tokens_out, head_out,
    acc_ref, recv_ref, direct_ref, h_acc, h_recv, z_ref, z_recv,
    r_send, r_recv, h_send, h_rsem, z_send, z_rsem,
):
    me = lax.axis_index("expert")
    row = lax.axis_index("dp")
    greet(count, dp_count)

    def cut_head(ref, piece):
        width = ref.shape[-1] // PIECES
        return ref.at[:, :, pl.ds(piece * width, width)]

    def cut_work(ref, piece):
        return columns(ref, piece, WORK_PIECES)

    head = Scatter(
        count, lambda m: head_ref.at[:, flip(me, m)], lambda m: h_acc.at[m // 2], h_recv, h_send, h_rsem, cut_head
    )
    work = Scatter(
        count, lambda m: partial_ref.at[m], lambda m: acc_ref.at[m // 2], recv_ref, r_send, r_recv, cut_work, WORK_PIECES
    )
    for piece in range(PIECES):
        head.send(0, piece)
    sends = []

    def head_step(step):
        last = step == head.steps() - 1
        for piece in range(PIECES):
            result = head.fold(step, piece)
            if last:
                target = cut_head(z_ref, piece)
                target[...] = result.astype(z_ref.dtype)
            else:
                head.send(step + 1, piece)
        if last:
            for offset in range(1, dp_count):
                other = lax.rem(row + offset, jnp.int32(dp_count))
                copy = pltpu.make_async_remote_copy(
                    src_ref=z_ref.at[other],
                    dst_ref=z_recv.at[offset],
                    send_sem=z_send.at[offset],
                    recv_sem=z_rsem.at[offset],
                    device_id={"dp": other},
                    device_id_type=MESH,
                )
                copy.start()
                sends.append(copy)

    def work_step(step, piece):
        result = work.fold(step, piece)
        if step == work.steps() - 1:
            width = tokens_out.shape[1] // WORK_PIECES
            cols = pl.ds(piece * width, width)
            tokens_out[:, cols] = (direct_ref[:, cols] + result).astype(tokens_out.dtype)
        else:
            work.send(step + 1, piece)

    for piece in range(WORK_PIECES):
        work.send(0, piece)
    for step in range(work.steps()):
        head_step(step)
        for piece in range(WORK_PIECES):
            work_step(step, piece)
        if step == 0:
            direct_ref[...] = lax.dot_general(
                grads_ref[0], projection_ref[...], CONTRACT_COLS, preferred_element_type=jnp.float32
            )
    total = z_ref[row].astype(jnp.float32)
    for offset, copy in enumerate(sends, 1):
        copy.wait_recv()
        total = total + z_recv[offset].astype(jnp.float32)
    head_out[...] = total * scale
    for copy in sends:
        copy.wait_send()
    head.finish()
    work.finish()


def vmem(count):
    return [pl.BlockSpec(memory_space=pltpu.VMEM)] * count


def params(number):
    return pltpu.CompilerParams(
        collective_id=number, has_side_effects=True, vmem_limit_bytes=VMEM_LIMIT
    )


def dma(*shape):
    return pltpu.SemaphoreType.DMA(shape)


def body(tokens, routes, gates, gate_up, down_proj, projection, matches):
    rows, width = tokens.shape
    top_k = routes.shape[1]
    count = lax.axis_size("expert")
    dp_count = lax.axis_size("dp")
    capacity = -(-(rows * top_k * 5 // (count * 4)) // 16) * 16
    slots = count * capacity
    hidden_width = down_proj.shape[1]
    embed = projection.shape[1]
    me = lax.axis_index("expert")
    bf16 = jnp.bfloat16
    f32 = jnp.float32
    weights_joined = gate_up[0]
    weights_down = down_proj[0]
    meta = jnp.concatenate(
        [routes.astype(f32).T, gates.T, matches.astype(f32)], axis=0
    )
    meta = jnp.pad(meta, ((0, -meta.shape[0] % 8), (0, 0)))
    everyone, metas = pl.pallas_call(
        functools.partial(gather_kernel, count),
        out_shape=(
            jax.ShapeDtypeStruct((count, rows, width), bf16),
            jax.ShapeDtypeStruct((count,) + meta.shape, f32),
        ),
        in_specs=vmem(2),
        out_specs=tuple(vmem(2)),
        scratch_shapes=[
            dma(PIECES, count), dma(PIECES, count), dma(1, count), dma(1, count), dma(2),
        ],
        compiler_params=params(0),
        name="gather_tokens",
    )(tokens, meta)
    chosen = metas[:, :top_k, :] == me.astype(f32)
    member = jnp.any(chosen, axis=1)
    gate_rows = jnp.sum(jnp.where(chosen, metas[:, top_k:2 * top_k, :], 0.0), axis=1)
    earlier = (jnp.arange(rows)[:, None] < jnp.arange(rows)[None, :]).astype(bf16)
    position = jnp.dot(member.astype(bf16), earlier, preferred_element_type=f32)
    slot_range = jnp.arange(capacity, dtype=jnp.int32).astype(f32)
    chooser = (
        member[:, None, :] & (position[:, None, :] == slot_range[None, :, None])
    ).astype(bf16)
    flat_input = jnp.einsum("scr,srd->scd", chooser, everyone, preferred_element_type=f32)
    flat_input = flat_input.astype(bf16).reshape(slots, width)
    joined = jnp.dot(flat_input, weights_joined, preferred_element_type=f32)
    hidden = (jax.nn.silu(joined[:, :hidden_width]) * joined[:, hidden_width:]).astype(bf16)
    outputs = jnp.dot(hidden, weights_down, preferred_element_type=f32).astype(bf16)
    projected = jnp.dot(outputs, projection, preferred_element_type=f32).astype(bf16)
    spread = jnp.einsum(
        "scr,sce->sre", chooser, projected.reshape(count, capacity, embed),
        preferred_element_type=f32,
    )
    partial = (gate_rows[:, :, None] * spread).astype(bf16)
    coefficient = 1.0 / (embed * TEMPER)
    half = max(1, count // 2)
    all_grads, loss = pl.pallas_call(
        functools.partial(middle_kernel, count, coefficient, 2 * top_k),
        out_shape=(
            jax.ShapeDtypeStruct((count, rows, embed), bf16),
            jax.ShapeDtypeStruct((1, rows), f32),
        ),
        in_specs=vmem(4),
        out_specs=tuple(vmem(2)),
        scratch_shapes=[
            pltpu.VMEM((half, rows, embed), bf16),
            pltpu.VMEM((count, rows, embed), bf16),
            pltpu.VMEM((rows, embed), bf16),
            pltpu.VMEM((rows, embed), bf16),
            pltpu.VMEM((rows, embed), bf16),
            dma(PIECES, count), dma(PIECES, count), dma(2),
            dma(PIECES, count), dma(PIECES, count), dma(1),
        ],
        compiler_params=params(1),
        name="contrast",
    )(partial, tokens, projection, metas)
    embed_grad = all_grads[0]
    gated = (gate_rows[:, :, None] * all_grads.astype(f32)).astype(bf16)
    slot_grads = jnp.einsum("scr,sre->sce", chooser, gated, preferred_element_type=f32)
    slot_grads = slot_grads.astype(bf16).reshape(slots, embed)
    output_grads = lax.dot_general(
        slot_grads, projection, CONTRACT_COLS, preferred_element_type=f32
    ).astype(bf16)
    hidden_grad = lax.dot_general(
        output_grads, weights_down, CONTRACT_COLS, preferred_element_type=f32
    )
    gate_act = joined[:, :hidden_width]
    up_act = joined[:, hidden_width:]
    sigmoid = jax.nn.sigmoid(gate_act)
    joined_grad = jnp.concatenate(
        [
            hidden_grad * up_act * sigmoid * (1.0 + gate_act * (1.0 - sigmoid)),
            hidden_grad * gate_act * sigmoid,
        ],
        axis=1,
    ).astype(bf16)
    input_grads = lax.dot_general(
        joined_grad, weights_joined, CONTRACT_COLS, preferred_element_type=f32
    ).astype(bf16)
    back = jnp.einsum(
        "scr,scd->srd", chooser, input_grads.reshape(count, capacity, width),
        preferred_element_type=f32,
    ).astype(bf16)
    head = lax.dot_general(tokens, embed_grad, CONTRACT_ROWS, preferred_element_type=f32)
    head = head + lax.dot_general(outputs, slot_grads, CONTRACT_ROWS, preferred_element_type=f32)
    share = width // (count * dp_count)
    head = head.astype(bf16).reshape(dp_count, count, share, embed)
    scale = 1.0 / math.sqrt(rows * count * dp_count)
    grad_tokens, grad_projection = pl.pallas_call(
        functools.partial(scatter_kernel, count, dp_count, scale),
        out_shape=(
            jax.ShapeDtypeStruct((rows, width), bf16),
            jax.ShapeDtypeStruct((share, embed), f32),
        ),
        in_specs=vmem(4),
        out_specs=tuple(vmem(2)),
        scratch_shapes=[
            pltpu.VMEM((half, rows, width), bf16),
            pltpu.VMEM((count, rows, width), bf16),
            pltpu.VMEM((rows, width), f32),
            pltpu.VMEM((half, dp_count, share, embed), bf16),
            pltpu.VMEM((count, dp_count, share, embed), bf16),
            pltpu.VMEM((dp_count, share, embed), bf16),
            pltpu.VMEM((dp_count, share, embed), bf16),
            dma(WORK_PIECES, count), dma(WORK_PIECES, count),
            dma(PIECES, count), dma(PIECES, count),
            dma(dp_count), dma(dp_count),
        ],
        compiler_params=params(2),
        name="scatter_grads",
    )(back, head, all_grads, projection)
    return (grad_tokens, grad_projection, loss.reshape(rows))


def solution(mesh):
    placed = (
        P(("dp", "expert"), None),
        P(("dp", "expert"), None),
        P(("dp", "expert"), None),
        P("expert", None, None),
        P("expert", None, None),
        P(),
        P(("dp", "expert"), None),
    )
    return jax.shard_map(
        body,
        mesh=mesh,
        in_specs=placed,
        out_specs=(P(("dp", "expert"), None), P(("dp", "expert"), None), P(("dp", "expert"))),
        check_vma=False,
    )
```
